32 devices in a mesh: dp: 4 (over x, core), expert: 8 (over z, y).
Axes of the slice: x: 2, y: 2, z: 4, core: 2. Of those that a mesh axis runs over, the one named last changes fastest.
Arguments:
- tokens: bfloat16 [2, 2048, 2048], P(None, ('dp', 'expert')), may hold values from -6 to 6
- cotangent: bfloat16 [2, 2048, 2048], P(None, ('dp', 'expert')), may hold values from -6 to 6
- segment_ids: int32 [2, 2048], replicated, may hold values from 0 to 9, as said below
- routes: int32 [2, 2048, 6], P(None, ('dp', 'expert')), may hold values from 0 to 15, all different within a row; in each aligned block of 64 rows (0 to 63, 64 to 127, ..., all dimensions but the last counted through in order) at most 30 rows name the same one
- norm_attn: bfloat16 [2048], P(('dp', 'expert')), may hold values from 0.5 to 1.5
- w_query: bfloat16 [2048, 3072], P(('dp', 'expert')), may hold values from -0.125 to 0.125
- w_kv_down: bfloat16 [2048, 576], P(('dp', 'expert')), may hold values from -0.125 to 0.125
- norm_latent: bfloat16 [512], P(('dp', 'expert')), may hold values from 0.5 to 1.5
- w_kv_up: bfloat16 [512, 4096], P(('dp', 'expert')), may hold values from -0.25 to 0.25
- w_out: bfloat16 [2048, 2048], P(None, ('dp', 'expert')), may hold values from -3 to 3
- norm_moe: bfloat16 [2048], P(('dp', 'expert')), may hold values from 0.5 to 1.5
- w_router: bfloat16 [2048, 16], P(('dp', 'expert')), may hold values from -0.125 to 0.125
- w_shared_gate: bfloat16 [2048, 2816], P('dp', 'expert'), may hold values from -0.125 to 0.125
- w_shared_up: bfloat16 [2048, 2816], P('dp', 'expert'), may hold values from -0.125 to 0.125
- w_shared_down: bfloat16 [2816, 2048], P('expert', 'dp'), may hold values from -0.109375 to 0.109375
- w_expert_gate: bfloat16 [16, 2048, 1408], P('expert', 'dp'), may hold values from -0.125 to 0.125
- w_expert_up: bfloat16 [16, 2048, 1408], P('expert', 'dp'), may hold values from -0.125 to 0.125
- w_expert_down: bfloat16 [16, 1408, 2048], P('expert', None, 'dp'), may hold values from -0.15625 to 0.15625
Outputs:
- block_out: bfloat16 [2, 2048, 2048], P(None, ('dp', 'expert'))
- grad_tokens: bfloat16 [2, 2048, 2048], P(None, ('dp', 'expert'))
- grad_norm_attn: float32 [2048], P(('dp', 'expert'))
- grad_w_query: float32 [2048, 3072], P(('dp', 'expert'))
- grad_w_kv_down: float32 [2048, 576], P(('dp', 'expert'))
- grad_norm_latent: float32 [512], P(('dp', 'expert'))
- grad_w_kv_up: float32 [512, 4096], P(('dp', 'expert'))
- grad_w_out: float32 [2048, 2048], P(None, ('dp', 'expert'))
- grad_norm_moe: float32 [2048], P(('dp', 'expert'))
- grad_w_router: float32 [2048, 16], P(('dp', 'expert'))
- grad_w_shared_gate: float32 [2048, 2816], P('dp', 'expert')
- grad_w_shared_up: float32 [2048, 2816], P('dp', 'expert')
- grad_w_shared_down: float32 [2816, 2048], P('expert', 'dp')
- grad_w_expert_gate: float32 [16, 2048, 1408], P('expert', 'dp')
- grad_w_expert_up: float32 [16, 2048, 1408], P('expert', 'dp')
- grad_w_expert_down: float32 [16, 1408, 2048], P('expert', None, 'dp')
The draws below stay inside these ranges and needn't reach their ends.
Inputs may be any that keep to these rules, and one draw needn't show every extreme that they name: `segment_ids`: each micro-batch is made of groups of 512 consecutive rows, each packed with whole sequences in order; numbers start at 0 and rise by one at each new sequence, so no number spans two groups. The first group of each micro-batch begins with a sequence of exactly 512 tokens, followed by 3 more if tokens remain; every other group holds 3 sequences; none has more than 512 tokens. `routes`: each token names 6 different experts in a fixed order; among the 64 tokens of one device in one micro-batch no expert is named more than 30 times.
All inputs are finite; a program needn't handle non-finite values.
Results may differ from the reference program's by a relative error of at most 0.023.
Values may be sent and summed in bfloat16 or wider, within the bound.
No kernel may reach another device: no remote copies, remote signals or barrier semaphores. Data moves between devices by JAX's collectives and lax.ppermute only.
A program may use at most 384 MiB of HBM per device.

```python
import math
import jax
import jax.numpy as jnp
import numpy as np
from jax import lax

D = 2048
HEADS = 16
NOPE = 128
ROPE = 64
VDIM = 128
LATENT = 512
FF = 1408
SHARED = 2816
TOPK = 6
MICRO = 2
PIECES = 3
TOK_MB = 64
EXPERTS = 16
NT = 2048
GROUP_TOK = 512
LEN0 = 512
CAP = 30
DEVICES = 32


def draw_segment_ids(key, part):
    group_count = NT // GROUP_TOK
    token_index = jnp.arange(GROUP_TOK, dtype=jnp.int32)
    micro_rows = []
    for micro_index in range(MICRO):
        group_rows = []
        offset = 0
        for group_index in range(group_count):
            head_length = LEN0 if group_index == 0 else 0
            remaining = GROUP_TOK - head_length
            if remaining == 0:
                local_ids = jnp.zeros((GROUP_TOK,), jnp.int32)
                seq_count = 1
            else:
                piece_step = remaining // PIECES
                jitter_reach = piece_step // 6
                group_key = jax.random.fold_in(key, micro_index * 1000 + group_index + 11)
                jitter = jax.random.randint(group_key, (PIECES,), -jitter_reach, jitter_reach + 1, dtype=jnp.int32)
                inner_bounds = (head_length + piece_step * jnp.arange(1, PIECES, dtype=jnp.int32) + jitter[:PIECES - 1]).astype(jnp.int32)
                if head_length > 0:
                    bounds = jnp.concatenate([jnp.full((1,), head_length, jnp.int32), inner_bounds])
                    seq_count = 1 + PIECES
                else:
                    bounds = inner_bounds
                    seq_count = PIECES
                local_ids = jnp.sum((token_index[:, None] >= bounds[None, :]).astype(jnp.int32), axis=1)
            group_rows.append(local_ids + offset)
            offset = offset + seq_count
        micro_rows.append(jnp.concatenate(group_rows))
    return jnp.stack(micro_rows).astype(jnp.int32)


def steps_of(key, shape, cuts, least, largest):
    loudness, own = 1.0, jax.random.fold_in(key, 6)
    for dim, blocks in cuts:
        steps = jnp.exp(jax.random.uniform(jax.random.fold_in(own, dim), (blocks,), jnp.float32, least / len(cuts), largest / len(cuts)))
        loudness = loudness * jnp.repeat(steps, shape[dim] // blocks).reshape([-1 if axis == dim else 1 for axis in range(len(shape))])
    return loudness


def assign_block(stream_key, own, number, rows, count, top, reach, skew):
    ranking = jax.random.permutation(stream_key, count)
    heavy_load, common = portions_of(count, rows * top, reach, skew, True), portions_of(count, rows * top, reach, skew, False)
    places = jnp.arange(count)

    def named(sizes, offset_by):
        used = int((sizes > 0).sum())
        fixed = max(1, used // 4)
        passed = fixed + (places - fixed + offset_by * (used - fixed)) % max(1, count - fixed)
        return jnp.zeros((count,), jnp.int32).at[ranking[jnp.where(places < fixed, places, passed)]].set(jnp.asarray(sizes, jnp.int32))

    sizes = jnp.where(number % 4 == 0, named(heavy_load, number // 4), named(common, number - number // 4 - 1))
    mixed = jax.random.permutation(jax.random.fold_in(own, 3), count)
    donor, taker = mixed[0:count // 2 * 2:2], mixed[1:count // 2 * 2:2]
    margin = jnp.minimum(sizes[donor] - 1, reach - sizes[taker]) // 2
    margin = jnp.where((donor == ranking[0]) | (taker == ranking[0]) | (sizes[taker] == 0), 0, jnp.maximum(margin, 0))
    passed = jax.random.randint(jax.random.fold_in(own, 4), (count // 2,), 0, 1 << 20) % (margin + 1)
    sizes = sizes.at[donor].add(-passed).at[taker].add(passed)
    members = jnp.searchsorted(jnp.cumsum(sizes), jnp.arange(rows * top), side="right").astype(jnp.int32)
    grid = members.reshape(top, rows).T
    grid = grid[jax.random.permutation(jax.random.fold_in(own, 1), rows)]
    offset_by = jax.random.randint(jax.random.fold_in(own, 2), (rows, 1), 0, top)
    return jnp.take_along_axis(grid, (jnp.arange(top)[None, :] + offset_by) % top, axis=1)


def portions_of(number_of, total, most, skew, full):
    loads = [(1 << 20) // math.isqrt(grade ** skew) + 1 for grade in range(1, number_of + 1)]
    largest = most if full else min(most, max(-(-total // number_of), total * loads[0] // sum(loads)))
    least = 1 if total - largest >= number_of - 1 else 0
    holding, surplus = [largest] + [least] * (number_of - 1), total - largest - least * (number_of - 1)
    while surplus > 0:
        free = [i for i in range(1, number_of) if holding[i] < largest] or [i for i in range(1, number_of) if holding[i] < most]
        whole, left = sum([loads[i] for i in free]), surplus
        for i in free:
            more = min(most - holding[i], max(1, left * loads[i] // whole), surplus)
            holding[i] = holding[i] + more
            surplus = surplus - more
    return np.array(holding)


def centred(key, dims, spread, limit, split=(), kind=jnp.bfloat16):
    level = steps_of(key, dims, split, -0.22, 0.18) if split else 1.0
    result = jax.random.normal(key, dims, jnp.float32) * spread * level
    return jnp.minimum(jnp.maximum(result, -limit), limit).astype(kind)


def setup_inputs(seed: int = 0) -> dict:
    splits = jax.random.split(jax.random.key(seed), 19)
    tokens = centred(splits[0], (MICRO, NT, D), 1.0, 6.0, ((1, 32),))
    cotangent = centred(splits[1], (MICRO, NT, D), 1.0, 6.0, ((1, 32),))
    segment_ids = draw_segment_ids(jax.random.fold_in(splits[18], 71), 0)
    routes_keys = jax.random.split(jax.random.fold_in(splits[3], 1), MICRO * NT // TOK_MB)
    routes_turns = jax.random.permutation(jax.random.fold_in(splits[3], 3), MICRO * NT // TOK_MB)
    routes = jax.vmap(lambda own, number: assign_block(jax.random.fold_in(splits[3], 2), own, number, TOK_MB, EXPERTS, TOPK, CAP, 2))(routes_keys, routes_turns).reshape((MICRO, NT, TOPK))
    norm_attn = jnp.clip(1.0 + 0.1 * jax.random.normal(splits[4], (D,), jnp.float32), 0.5, 1.5).astype(jnp.bfloat16)
    w_query = centred(splits[5], (D, HEADS * (NOPE + ROPE)), D ** -0.5, 0.125, ((0, 32),))
    w_kv_down = centred(splits[6], (D, LATENT + ROPE), D ** -0.5, 0.125, ((0, 32),))
    norm_latent = jnp.clip(1.0 + 0.1 * jax.random.normal(splits[7], (LATENT,), jnp.float32), 0.5, 1.5).astype(jnp.bfloat16)
    w_kv_up = centred(splits[8], (LATENT, HEADS * (NOPE + VDIM)), LATENT ** -0.5, 0.25, ((0, 32),))
    w_out = centred(splits[9], (HEADS * VDIM, D), (max(1, HEADS * VDIM // 512)) ** -0.5, 3.0, ((1, 32),))
    norm_moe = jnp.clip(1.0 + 0.1 * jax.random.normal(splits[10], (D,), jnp.float32), 0.5, 1.5).astype(jnp.bfloat16)
    w_router = centred(splits[11], (D, EXPERTS), D ** -0.5, 0.125, ((0, 32),))
    w_shared_gate = centred(splits[12], (D, SHARED), D ** -0.5, 0.125, ((0, 4), (1, 8)))
    w_shared_up = centred(splits[13], (D, SHARED), D ** -0.5, 0.125, ((0, 4), (1, 8)))
    w_shared_down = centred(splits[14], (SHARED, D), SHARED ** -0.5, 0.109375, ((0, 8), (1, 4)))
    w_expert_gate = centred(splits[15], (EXPERTS, D, FF), D ** -0.5, 0.125, ((0, 8), (1, 4)))
    w_expert_up = centred(splits[16], (EXPERTS, D, FF), D ** -0.5, 0.125, ((0, 8), (1, 4)))
    w_expert_down = centred(splits[17], (EXPERTS, FF, D), FF ** -0.5, 0.15625, ((0, 8), (2, 4)))
    return {"tokens": tokens, "cotangent": cotangent, "segment_ids": segment_ids, "routes": routes, "norm_attn": norm_attn, "w_query": w_query, "w_kv_down": w_kv_down, "norm_latent": norm_latent, "w_kv_up": w_kv_up, "w_out": w_out, "norm_moe": norm_moe, "w_router": w_router, "w_shared_gate": w_shared_gate, "w_shared_up": w_shared_up, "w_shared_down": w_shared_down, "w_expert_gate": w_expert_gate, "w_expert_up": w_expert_up, "w_expert_down": w_expert_down}


@jax.custom_vjp
def low(v):
    return lax.optimization_barrier(v.astype(jnp.bfloat16)).astype(jnp.float32)

@jax.custom_vjp
def low_back(v):
    return v

def low_keep(v):
    return (low(v), None)

def low_pass(kept, grad):
    return (grad,)

def back_keep(v):
    return (v, None)

def back_low(kept, grad):
    return (low(grad),)
low.defvjp(low_keep, low_pass)
low_back.defvjp(back_keep, back_low)

def round_both(values):
    return low_back(low(values))

def product(left, right):
    return jnp.dot(left, right, precision=lax.Precision.HIGHEST, preferred_element_type=jnp.float32)

def einsum_high(formula, left, right):
    return jnp.einsum(formula, left, right, precision=lax.Precision.HIGHEST, preferred_element_type=jnp.float32)

def rms_scale(values, gain):
    inverse = lax.rsqrt(lax.optimization_barrier(jnp.mean(values * values, axis=-1, keepdims=True)) + 1e-06)
    return values * inverse * gain

def silu_act(values):
    return values * (1.0 / (1.0 + jnp.exp(-values)))

def rotate(values, angle_table):
    half_width = values.shape[-1] // 2
    cosine = jnp.cos(angle_table)
    sine = jnp.sin(angle_table)
    first_half = values[..., :half_width]
    second_half = values[..., half_width:]
    return jnp.concatenate([first_half * cosine - second_half * sine, second_half * cosine + first_half * sine], axis=-1)

def block_forward(residual_in, segments, route_table, norm_attn, w_query, w_kv_down, norm_latent, w_kv_up, w_out, norm_moe, w_router, w_shared_gate, w_shared_up, w_shared_down, w_expert_gate, w_expert_up, w_expert_down):
    token_count = residual_in.shape[0]
    expert_total = w_router.shape[1]
    normed_attn = low(rms_scale(residual_in, norm_attn))
    query = round_both(product(normed_attn, w_query)).reshape(token_count, HEADS, NOPE + ROPE)
    latent_down = low_back(product(normed_attn, w_kv_down))
    latent = low(rms_scale(latent_down[:, :LATENT], norm_latent))
    positions = jnp.arange(token_count, dtype=jnp.float32)
    frequency = 10000.0 ** (-jnp.arange(ROPE // 2, dtype=jnp.float32) / (ROPE // 2))
    angle_table = positions[:, None] * frequency[None, :]
    key_rotary = low(rotate(latent_down[:, LATENT:], angle_table))
    query_rotary = low(rotate(query[:, :, NOPE:], angle_table[:, None, :]))
    up_heads = w_kv_up.reshape(LATENT, HEADS, NOPE + VDIM)
    query_lat = round_both(einsum_high('thn,lhn->thl', query[:, :, :NOPE], up_heads[:, :, :NOPE]))
    score_scale = (NOPE + ROPE) ** (-0.5)
    block_width = min(512, token_count)
    block_count = token_count // block_width
    key_index = jnp.arange(token_count, dtype=jnp.int32)

    def attend(block_args):
        block_lat, block_rot, block_segments, block_index = block_args
        raw_scores = low_back(einsum_high('qhl,kl->qhk', block_lat, latent) + einsum_high('qhr,kr->qhk', block_rot, key_rotary))
        valid_mask = (block_segments[:, None] == segments[None, :]) & (key_index[None, :] <= block_index[:, None])
        scores = jnp.where(valid_mask[:, None, :], raw_scores * score_scale, -1e+30)
        maximum = lax.optimization_barrier(jnp.max(scores, axis=-1, keepdims=True))
        log_total = maximum + jnp.log(lax.optimization_barrier(jnp.sum(jnp.exp(scores - maximum), axis=-1, keepdims=True)))
        weights = low(jnp.exp(scores - log_total))
        return round_both(einsum_high('qhk,kl->qhl', weights, latent))
    attended = lax.map(jax.checkpoint(attend), (query_lat.reshape(block_count, block_width, HEADS, LATENT), query_rotary.reshape(block_count, block_width, HEADS, ROPE), segments.reshape(block_count, block_width), key_index.reshape(block_count, block_width)))
    attended = attended.reshape(token_count, HEADS, LATENT)
    heads_out = round_both(einsum_high('thl,lhv->thv', attended, up_heads[:, :, NOPE:])).reshape(token_count, HEADS * VDIM)
    middle = residual_in + low_back(product(heads_out, w_out))
    normed_moe = low(rms_scale(middle, norm_moe))
    logits = low_back(product(normed_moe, w_router))
    exp_logits = jnp.exp(logits - lax.optimization_barrier(jnp.max(logits, axis=-1, keepdims=True)))
    router_probs = exp_logits / lax.optimization_barrier(jnp.sum(exp_logits, axis=-1, keepdims=True))
    gate_values = jnp.take_along_axis(router_probs, route_table, axis=1)
    shared_hidden = round_both(silu_act(low_back(product(normed_moe, w_shared_gate))) * low_back(product(normed_moe, w_shared_up)))
    shared_out = low_back(product(shared_hidden, w_shared_down))
    flat_routes = route_table.reshape(-1)
    route_hot = (flat_routes[:, None] == jnp.arange(expert_total, dtype=jnp.int32)[None, :]).astype(jnp.int32)
    slot_rank = lax.optimization_barrier(jnp.sum((jnp.cumsum(route_hot, axis=0) - route_hot) * route_hot, axis=1))
    capacity_all = CAP * DEVICES
    slot_index = (flat_routes * capacity_all + slot_rank).astype(jnp.int32)
    source_row = jnp.repeat(jnp.arange(token_count, dtype=jnp.int32), TOPK)
    dispatched = jnp.zeros((expert_total * capacity_all, D), jnp.float32).at[slot_index].set(normed_moe[source_row])
    dispatched = dispatched.reshape(expert_total, capacity_all, D)

    def expert(expert_args):
        expert_rows, gate_weight, up_weight, down_weight = expert_args
        hidden_act = round_both(silu_act(low_back(product(expert_rows, gate_weight))) * low_back(product(expert_rows, up_weight)))
        return round_both(product(hidden_act, down_weight))
    results = lax.map(jax.checkpoint(expert), (dispatched, w_expert_gate, w_expert_up, w_expert_down))
    picked_rows = results.reshape(expert_total * capacity_all, D)[slot_index].reshape(token_count, TOPK, D)
    routed_sum = lax.optimization_barrier(jnp.sum(gate_values[:, :, None] * picked_rows, axis=1))
    return middle + shared_out + routed_sum

def reference(tokens, cotangent, segment_ids, routes, norm_attn, w_query, w_kv_down, norm_latent, w_kv_up, w_out, norm_moe, w_router, w_shared_gate, w_shared_up, w_shared_down, w_expert_gate, w_expert_up, w_expert_down):
    weight_list = (norm_attn, w_query, w_kv_down, norm_latent, w_kv_up, w_out, norm_moe, w_router, w_shared_gate, w_shared_up, w_shared_down, w_expert_gate, w_expert_up, w_expert_down)
    weight_values = tuple((weight.astype(jnp.float32) for weight in weight_list))
    grad_totals = tuple((jnp.zeros(weight.shape, jnp.float32) for weight in weight_list))
    outputs = []
    input_grads = []
    for micro_index in range(MICRO):
        segments = segment_ids[micro_index]
        route_table = routes[micro_index]

        def forward(residual_in, *weights):
            return block_forward(residual_in, segments, route_table, *weights)
        block_out, pullback = jax.vjp(forward, tokens[micro_index].astype(jnp.float32), *weight_values)
        pulled = pullback(cotangent[micro_index].astype(jnp.float32))
        outputs.append(block_out.astype(jnp.bfloat16))
        input_grads.append(pulled[0].astype(jnp.bfloat16))
        grad_totals = tuple((total + extra for total, extra in zip(grad_totals, pulled[1:])))
    return (jnp.stack(outputs), jnp.stack(input_grads), grad_totals[0], grad_totals[1], grad_totals[2], grad_totals[3], grad_totals[4], grad_totals[5], grad_totals[6], grad_totals[7], grad_totals[8], grad_totals[9], grad_totals[10], grad_totals[11], grad_totals[12], grad_totals[13])
```

```python
import jax
import jax.numpy as jnp
from jax import lax
from jax.sharding import PartitionSpec as P

NOPE = 128
ROPE = 64
VDIM = 128
QDIM = NOPE + ROPE
KVDIM = NOPE + VDIM
EPS = 1e-06


f32 = jnp.float32
bf16 = jnp.bfloat16


def ring_order(count):
    return (0, 2, 4, 6, 7, 5, 3, 1) if count == 8 else tuple(range(count))


def ring_pairs(count, step):
    order = ring_order(count)
    return [(order[i], order[(i + step) % count]) for i in range(count)]


def ring_gather(chunk, count):
    pieces = [None] * count
    pieces[0] = ahead = behind = chunk
    for step in range(1, count // 2 + 1):
        ahead = lax.ppermute(ahead, "expert", ring_pairs(count, -1))
        pieces[step] = ahead
        if step < count - count // 2:
            behind = lax.ppermute(behind, "expert", ring_pairs(count, 1))
            pieces[count - step] = behind
    return pieces


def ring_scatter(parts, count):
    ahead_steps = count // 2
    behind_steps = count - 1 - ahead_steps
    carry = parts[ahead_steps]
    back = parts[count - behind_steps] if behind_steps else None
    for step in range(ahead_steps):
        carry = lax.ppermute(carry, "expert", ring_pairs(count, 1))
        left = ahead_steps - 1 - step
        if left:
            carry = (carry.astype(f32) + parts[left].astype(f32)).astype(bf16)
        if step < behind_steps:
            back = lax.ppermute(back, "expert", ring_pairs(count, -1))
            left = behind_steps - 1 - step
            if left:
                back = (back.astype(f32) + parts[count - left].astype(f32)).astype(bf16)
    total = parts[0].astype(f32) + carry.astype(f32)
    return total + back.astype(f32) if behind_steps else total


def swap_pairs(count, bit):
    return [(i, i ^ bit) for i in range(count)]


def dp_gather(shard, count):
    held = {0: shard}
    bit = count // 2
    while bit:
        for k in list(held):
            held[k ^ bit] = lax.ppermute(held[k], "dp", swap_pairs(count, bit))
        bit //= 2
    return [held[k] for k in range(count)]


def dp_scatter(parts, count):
    held = dict(enumerate(parts))
    bit = 1
    while bit < count:
        kept = {}
        for k in held:
            if not k & bit:
                received = lax.ppermute(held[k | bit], "dp", swap_pairs(count, bit))
                kept[k] = held[k].astype(f32) + received.astype(f32)
        bit *= 2
        held = kept if bit >= count else {k: v.astype(bf16) for k, v in kept.items()}
    return held[0]


def dp_assemble(pieces, axis):
    count = len(pieces)
    own = lax.axis_index("dp")
    width = pieces[0].shape[axis]
    shape = list(pieces[0].shape)
    shape[axis] = width * count
    whole = jnp.zeros(shape, pieces[0].dtype)
    for k, piece in enumerate(pieces):
        whole = lax.dynamic_update_slice_in_dim(whole, piece, (own ^ k) * width, axis)
    return whole


def dp_block(whole, k, count, axis):
    width = whole.shape[axis] // count
    return lax.dynamic_slice_in_dim(whole, (lax.axis_index("dp") ^ k) * width, width, axis)


def silu_parts(values):
    sigmoid = 1.0 / (1.0 + jnp.exp(-values))
    return values * sigmoid, sigmoid * (1.0 + values * (1.0 - sigmoid))


def norm_forward(values, gain):
    inverse = lax.rsqrt(jnp.mean(values * values, axis=-1, keepdims=True) + EPS)
    return values * inverse * gain, inverse


def norm_backward(values, inverse, gain, gradient):
    scaled = gradient * gain
    grad_gain = jnp.sum(gradient * values * inverse, axis=(0, 1))
    grad_values = inverse * scaled - values * inverse**3 * jnp.mean(
        values * scaled, axis=-1, keepdims=True
    )
    return grad_values, grad_gain


def rotate(values, cosine, sine, direction):
    half_width = values.shape[-1] // 2
    first_half = values[..., :half_width]
    second_half = values[..., half_width:]
    return jnp.concatenate(
        [
            first_half * cosine - direction * (second_half * sine),
            second_half * cosine + direction * (first_half * sine),
        ],
        axis=-1,
    )


def dot(formula, left, right):
    return jnp.einsum(formula, left, right, preferred_element_type=f32)


def per_device(
    tokens,
    cotangent,
    segment_ids,
    routes,
    norm_attn,
    w_query,
    w_kv_down,
    norm_latent,
    w_kv_up,
    w_out,
    norm_moe,
    w_router,
    w_shared_gate,
    w_shared_up,
    w_shared_down,
    w_expert_gate,
    w_expert_up,
    w_expert_down,
):
    micro, local, width = tokens.shape
    top = routes.shape[2]
    experts = w_router.shape[1]
    own_experts = w_expert_gate.shape[0]
    ring = lax.axis_size("expert")
    dp = lax.axis_size("dp")
    rows = w_query.shape[0]
    heads = w_query.shape[1] // QDIM
    lat_rows = norm_latent.shape[0]
    latent_width = lat_rows * ring * dp
    kv_width = w_kv_down.shape[1]
    shared_own = w_shared_gate.shape[1]
    group = local * ring
    capacity = max(2, 5 * local * top // (4 * experts))
    slots = ring * capacity
    score_scale = QDIM ** (-0.5)
    expert_index = lax.axis_index("expert")
    dp_index = lax.axis_index("dp")
    own_heads = max(1, heads // ring)
    sharers = max(1, ring // heads)
    head_groups = heads // own_heads
    part_len = local // sharers
    query_count = group // sharers

    order = ring_order(ring)
    place = {device: i for i, device in enumerate(order)}
    ahead_table = jnp.array(
        [[order[(place[d] + j) % ring] for j in range(ring)] for d in range(ring)], jnp.int32
    )
    ahead = lax.dynamic_slice_in_dim(ahead_table, expert_index, 1, 0)[0]
    back_table = jnp.array(
        [[(place[s] - place[d]) % ring for s in range(ring)] for d in range(ring)], jnp.int32
    )
    back = lax.dynamic_slice_in_dim(back_table, expert_index, 1, 0)[0]

    def chunk(values, j):
        return values[:, j * local : (j + 1) * local]

    def chunks(values):
        return [chunk(values, j) for j in range(ring)]

    def own_part(values):
        if sharers == 1:
            return values
        shaped = values.reshape((micro, ring, local) + values.shape[2:])
        part = lax.dynamic_slice_in_dim(
            shaped, (expert_index % sharers) * part_len, part_len, 2
        )
        return part.reshape((micro, query_count) + values.shape[2:])

    def whole_part(values):
        if sharers == 1:
            return values
        shaped = values.reshape((micro, ring, part_len) + values.shape[2:])
        blank = jnp.zeros((micro, ring, local) + values.shape[2:], values.dtype)
        filled = lax.dynamic_update_slice_in_dim(
            blank, shaped, (expert_index % sharers) * part_len, 2
        )
        return filled.reshape((micro, group) + values.shape[2:])

    group_tokens = jnp.concatenate(ring_gather(tokens, ring), axis=1)
    group_grad = jnp.concatenate(ring_gather(cotangent, ring), axis=1)

    up_cols = lat_rows * own_heads * KVDIM // rows
    flag_cols = micro * local * own_experts // rows
    lat_pad = jnp.zeros((rows - lat_rows, 1), bf16)

    def per_head(weight, head_width):
        split = weight.reshape(weight.shape[0], head_groups, own_heads * head_width)
        return jnp.repeat(jnp.transpose(split, (1, 0, 2)), sharers, axis=0)

    def to_all(weight):
        return jnp.broadcast_to(weight[None], (ring,) + weight.shape)

    named = jnp.sum(
        (routes[..., None] == jnp.arange(experts, dtype=jnp.int32)).astype(bf16), axis=2
    )
    flags = jnp.transpose(named.reshape(micro, local, ring, own_experts), (2, 0, 1, 3))
    fields = [
        per_head(w_query, QDIM),
        per_head(w_out.T, VDIM),
        per_head(w_kv_up, KVDIM).reshape(ring, rows, up_cols),
        to_all(w_kv_down),
        to_all(w_router),
        to_all(norm_attn[:, None]),
        to_all(norm_moe[:, None]),
        to_all(jnp.concatenate([norm_latent[:, None], lat_pad], axis=0)),
        flags.reshape(ring, rows, flag_cols),
    ]
    starts = [0]
    for field in fields:
        starts.append(starts[-1] + field.shape[2])
    pad = -starts[-1] % 128
    if pad:
        fields.append(jnp.zeros((ring, rows, pad), bf16))
    packed = jnp.concatenate(fields, axis=2)
    arrived = lax.all_to_all(packed, "expert", 0, 0, tiled=True)
    dense = dp_assemble([a[None] for a in dp_gather(arrived, dp)], 0)

    def field_of(number):
        return dense[..., starts[number] : starts[number + 1]]

    weight_query = field_of(0).reshape(width, own_heads * QDIM)
    weight_out = field_of(1).reshape(width, own_heads * VDIM)
    weight_up = field_of(2).reshape(latent_width, own_heads, KVDIM)
    up_key = weight_up[:, :, :NOPE]
    up_value = weight_up[:, :, NOPE:]
    weight_down = field_of(3).reshape(width, kv_width)
    weight_router = field_of(4).reshape(width, experts)
    gain_attn = field_of(5).reshape(width).astype(f32)
    gain_moe = field_of(6).reshape(width).astype(f32)
    gain_latent = field_of(7)[:, :, :lat_rows].reshape(latent_width).astype(f32)

    expert_gate = dp_assemble(dp_gather(w_expert_gate, dp), 1)
    expert_up = dp_assemble(dp_gather(w_expert_up, dp), 1)
    expert_down = dp_assemble(dp_gather(w_expert_down, dp), 2)
    shared_in = dp_assemble(
        dp_gather(jnp.concatenate([w_shared_gate, w_shared_up], axis=1), dp), 0
    )
    shared_gate_w = shared_in[:, :shared_own]
    shared_up_w = shared_in[:, shared_own:]
    shared_down_w = dp_assemble(dp_gather(w_shared_down, dp), 1)

    token_index = (
        (dp_index * ring + ahead)[:, None] * local + jnp.arange(local, dtype=jnp.int32)[None, :]
    ).reshape(group)
    frequency = 10000.0 ** (-jnp.arange(ROPE // 2, dtype=f32) / (ROPE // 2))
    angle_table = token_index.astype(f32)[:, None] * frequency[None, :]
    cosine = jnp.cos(angle_table)[None]
    sine = jnp.sin(angle_table)[None]
    group_ids = lax.dynamic_slice_in_dim(segment_ids, dp_index * group, group, 1)
    key_segments = jnp.take(group_ids.reshape(micro, ring, local), ahead, axis=1).reshape(
        micro, group
    )
    query_segments = own_part(key_segments)
    key_index = jnp.broadcast_to(token_index[None], (micro, group))
    query_index = own_part(key_index)
    query_cos = own_part(jnp.broadcast_to(cosine, (micro,) + cosine.shape[1:]))[:, :, None, :]
    query_sin = own_part(jnp.broadcast_to(sine, (micro,) + sine.shape[1:]))[:, :, None, :]
    valid = (query_segments[:, :, None] == key_segments[:, None, :]) & (
        key_index[:, None, :] <= query_index[:, :, None]
    )

    own_flags = arrived[..., starts[8] : starts[9]].reshape(ring, micro, local, own_experts)
    own_flags = jnp.transpose(jnp.take(own_flags, ahead, axis=0), (1, 0, 2, 3)).reshape(
        micro, group, own_experts
    )
    earlier = jnp.arange(group)[:, None] > jnp.arange(group)[None, :]
    rank = dot("ts,msx->mtx", earlier.astype(bf16), own_flags)
    rank = jnp.where(own_flags > 0, rank, -1.0).astype(jnp.int32)
    picks_bool = rank.transpose(0, 2, 1)[:, :, None, :] == jnp.arange(slots, dtype=jnp.int32)[
        None, None, :, None
    ]
    picks = picks_bool.astype(bf16)

    tokens_float = group_tokens.astype(f32)
    normed_float, inverse_group = norm_forward(tokens_float, gain_attn)
    normed_attn = normed_float.astype(bf16)
    normed_query = own_part(normed_attn)
    query = (
        dot("mtd,de->mte", normed_query, weight_query)
        .astype(bf16)
        .reshape(micro, query_count, own_heads, QDIM)
    )
    latent_down = dot("mtd,de->mte", normed_attn, weight_down)
    latent_pre = latent_down[..., :latent_width]
    latent_float, inverse_latent = norm_forward(latent_pre, gain_latent)
    latent = latent_float.astype(bf16)
    key_rotary = rotate(latent_down[..., latent_width:], cosine, sine, 1.0).astype(bf16)
    query_rot = rotate(query[..., NOPE:].astype(f32), query_cos, query_sin, 1.0).astype(bf16)
    query_full = jnp.concatenate([query[..., :NOPE], query_rot], axis=-1)
    key_nope = dot("mkl,lhn->mkhn", latent, up_key).astype(bf16)
    value = dot("mkl,lhv->mkhv", latent, up_value).astype(bf16)
    key_full = jnp.concatenate(
        [
            key_nope,
            jnp.broadcast_to(key_rotary[:, :, None, :], (micro, group, own_heads, ROPE)),
        ],
        axis=-1,
    )
    scores = jnp.where(
        valid[:, None], dot("mqhd,mkhd->mhqk", query_full, key_full) * score_scale, -1e30
    )
    top_score = jnp.max(scores, axis=-1, keepdims=True)
    unscaled = jnp.exp(scores - top_score)
    probs = unscaled / jnp.sum(unscaled, axis=-1, keepdims=True)
    probs_low = probs.astype(bf16)
    heads_out = (
        dot("mhqk,mkhv->mqhv", probs_low, value)
        .astype(bf16)
        .reshape(micro, query_count, own_heads * VDIM)
    )
    middle_part = whole_part(dot("mtv,dv->mtd", heads_out, weight_out).astype(bf16))
    own_tokens = tokens.astype(f32)
    middle = own_tokens + ring_scatter(chunks(middle_part), ring)
    moe_float, inverse_moe = norm_forward(middle, gain_moe)
    normed_moe = moe_float.astype(bf16)
    group_normed = jnp.concatenate(ring_gather(normed_moe, ring), axis=1)

    logits = dot("mtd,de->mte", group_normed, weight_router)
    exp_logits = jnp.exp(logits - jnp.max(logits, axis=-1, keepdims=True))
    router_probs = exp_logits / jnp.sum(exp_logits, axis=-1, keepdims=True)
    gate_values = lax.dynamic_slice_in_dim(
        router_probs, expert_index * own_experts, own_experts, 2
    )
    slot_gates = jnp.sum(
        jnp.where(picks_bool, gate_values.transpose(0, 2, 1)[:, :, None, :], 0.0), axis=-1
    )
    slot_gates = jnp.transpose(slot_gates, (1, 0, 2)).reshape(own_experts, micro * slots, 1)

    def to_slots(values):
        picked = dot("mxrt,mtd->xmrd", picks, values).astype(bf16)
        return picked.reshape(own_experts, micro * slots, width)

    def from_slots(values):
        return dot(
            "mxrt,xmrd->mtd", picks, values.reshape(own_experts, micro, slots, width)
        )

    slot_rows = to_slots(group_normed)
    slot_grads = to_slots(group_grad)
    gate_pre = dot("xrd,xdf->xrf", slot_rows, expert_gate)
    up_pre = dot("xrd,xdf->xrf", slot_rows, expert_up)
    grad_plain = dot("xrd,xfd->xrf", slot_grads, expert_down)
    gate_act, gate_slope = silu_parts(gate_pre)
    hidden = gate_act * up_pre
    hidden_scaled = (slot_gates * hidden).astype(bf16)
    slot_grad_gates = jnp.sum(hidden * grad_plain, axis=-1)
    grad_hidden = slot_gates * grad_plain
    grad_gate_rows = (grad_hidden * up_pre * gate_slope).astype(bf16)
    grad_up_rows = (grad_hidden * gate_act).astype(bf16)
    grad_down_parts = [
        dot("xrf,xrd->xfd", hidden_scaled, dp_block(slot_grads, k, dp, 2)).astype(bf16)
        for k in range(dp)
    ]
    grad_gate_parts = [
        dot("xrd,xrf->xdf", dp_block(slot_rows, k, dp, 2), grad_gate_rows).astype(bf16)
        for k in range(dp)
    ]
    grad_up_parts = [
        dot("xrd,xrf->xdf", dp_block(slot_rows, k, dp, 2), grad_up_rows).astype(bf16)
        for k in range(dp)
    ]
    grad_expert_down = dp_scatter(grad_down_parts, dp)
    grad_expert_gate = dp_scatter(grad_gate_parts, dp)
    grad_expert_up = dp_scatter(grad_up_parts, dp)
    slot_out = dot("xrf,xfd->xrd", hidden_scaled, expert_down).astype(bf16)
    slot_back = (
        dot("xrf,xdf->xrd", grad_gate_rows, expert_gate)
        + dot("xrf,xdf->xrd", grad_up_rows, expert_up)
    ).astype(bf16)

    shared_gate = dot("mtd,df->mtf", group_normed, shared_gate_w)
    shared_up = dot("mtd,df->mtf", group_normed, shared_up_w)
    shared_act, shared_slope = silu_parts(shared_gate)
    shared_hidden = (shared_act * shared_up).astype(bf16)
    grad_shared_hidden = dot("mtd,fd->mtf", group_grad, shared_down_w)
    grad_shared_gate = (grad_shared_hidden * shared_up * shared_slope).astype(bf16)
    grad_shared_up = (grad_shared_hidden * shared_act).astype(bf16)
    grad_shared_in = jnp.concatenate([grad_shared_gate, grad_shared_up], axis=-1)
    shared_in_parts = [
        dot("mtd,mtf->df", dp_block(group_normed, k, dp, 2), grad_shared_in).astype(bf16)
        for k in range(dp)
    ]
    shared_down_parts = [
        dot("mtf,mtd->fd", shared_hidden, dp_block(group_grad, k, dp, 2)).astype(bf16)
        for k in range(dp)
    ]
    grad_shared_in_w = dp_scatter(shared_in_parts, dp)
    grad_shared_down = dp_scatter(shared_down_parts, dp)

    out_part = (
        dot("mtf,fd->mtd", shared_hidden, shared_down_w) + from_slots(slot_out)
    ).astype(bf16)
    back_part = (
        dot("mtf,df->mtd", grad_shared_in, shared_in) + from_slots(slot_back)
    ).astype(bf16)
    grad_normed_moe = ring_scatter(chunks(back_part), ring)
    block_out = (middle + ring_scatter(chunks(out_part), ring)).astype(bf16)

    grad_gates = jnp.sum(
        jnp.where(
            picks_bool,
            jnp.transpose(slot_grad_gates.reshape(own_experts, micro, slots), (1, 0, 2))[..., None],
            0.0,
        ),
        axis=2,
    )
    grad_gates = jnp.transpose(grad_gates.reshape(micro, own_experts, ring, local), (2, 0, 3, 1))
    grad_gates = lax.all_to_all(
        jnp.take(grad_gates, back, axis=0), "expert", 0, 0, tiled=True
    )
    grad_probs = jnp.transpose(grad_gates, (1, 2, 0, 3)).reshape(micro, local, experts)
    own_probs = router_probs[:, :local]
    grad_logits = (
        own_probs * (grad_probs - jnp.sum(own_probs * grad_probs, axis=-1, keepdims=True))
    ).astype(bf16)
    grad_normed_moe = grad_normed_moe + dot("mte,de->mtd", grad_logits, weight_router)
    grad_router = dot("mtd,mte->de", normed_moe, grad_logits)
    grad_middle_norm, grad_gain_moe = norm_backward(middle, inverse_moe, gain_moe, grad_normed_moe)
    grad_middle = cotangent.astype(f32) + grad_middle_norm
    grad_middle_low = grad_middle.astype(bf16)

    group_middle = own_part(jnp.concatenate(ring_gather(grad_middle_low, ring), axis=1))
    grad_heads = (
        dot("mtd,dv->mtv", group_middle, weight_out)
        .astype(bf16)
        .reshape(micro, query_count, own_heads, VDIM)
    )
    grad_out_w = dot("mtd,mtv->dv", group_middle, heads_out)
    grad_value = dot("mhqk,mqhv->mkhv", probs_low, grad_heads).astype(bf16)
    grad_weights = dot("mqhv,mkhv->mhqk", grad_heads, value)
    delta = jnp.sum(probs * grad_weights, axis=-1, keepdims=True)
    grad_scores = (probs * (grad_weights - delta) * score_scale).astype(bf16)
    grad_query_full = dot("mhqk,mkhd->mqhd", grad_scores, key_full)
    grad_key_full = dot("mhqk,mqhd->mkhd", grad_scores, query_full)
    grad_key_nope = grad_key_full[..., :NOPE].astype(bf16)
    grad_key_rot_part = jnp.sum(grad_key_full[..., NOPE:], axis=2)
    grad_up_key = dot("mkl,mkhn->lhn", latent, grad_key_nope)
    grad_up_value = dot("mkl,mkhv->lhv", latent, grad_value)
    grad_latent_part = dot("mkhn,lhn->mkl", grad_key_nope, up_key) + dot(
        "mkhv,lhv->mkl", grad_value, up_value
    )
    grad_key_part = jnp.concatenate([grad_latent_part, grad_key_rot_part], axis=-1).astype(bf16)
    grad_key_own = ring_scatter(chunks(grad_key_part), ring)
    grad_query = (
        jnp.concatenate(
            [
                grad_query_full[..., :NOPE],
                rotate(grad_query_full[..., NOPE:], query_cos, query_sin, -1.0),
            ],
            axis=-1,
        )
        .astype(bf16)
        .reshape(micro, query_count, own_heads * QDIM)
    )
    grad_query_w = dot("mtd,mte->de", normed_query, grad_query)
    grad_normed_part = whole_part(dot("mte,de->mtd", grad_query, weight_query).astype(bf16))
    grad_normed_attn = ring_scatter(chunks(grad_normed_part), ring)
    grad_latent_pre, grad_gain_latent = norm_backward(
        chunk(latent_pre, 0), chunk(inverse_latent, 0), gain_latent, grad_key_own[..., :latent_width]
    )
    grad_down = jnp.concatenate(
        [
            grad_latent_pre,
            rotate(
                grad_key_own[..., latent_width:], chunk(cosine, 0), chunk(sine, 0), -1.0
            ),
        ],
        axis=-1,
    ).astype(bf16)
    grad_down_w = dot("mtd,mte->de", chunk(normed_attn, 0), grad_down)
    grad_normed_attn = grad_normed_attn + dot("mte,de->mtd", grad_down, weight_down)
    grad_input_norm, grad_gain_attn = norm_backward(
        own_tokens, chunk(inverse_group, 0), gain_attn, grad_normed_attn
    )
    grad_tokens = (grad_middle + grad_input_norm).astype(bf16)

    def by_owner(gradient):
        return gradient.astype(bf16).reshape(dp, ring, rows, -1)

    grad_up_w = jnp.concatenate([grad_up_key, grad_up_value], axis=-1)
    lat_blank = jnp.zeros((dp, ring, rows - lat_rows, 1), bf16)
    gradients = [
        by_owner(grad_query_w),
        by_owner(grad_out_w),
        by_owner(grad_up_w),
        by_owner(grad_down_w),
        by_owner(grad_router),
        by_owner(grad_gain_attn),
        by_owner(grad_gain_moe),
        jnp.concatenate(
            [grad_gain_latent.astype(bf16).reshape(dp, ring, lat_rows, 1), lat_blank], axis=2
        ),
    ]
    grad_starts = [0]
    for field in gradients:
        grad_starts.append(grad_starts[-1] + field.shape[3])
    pad = -grad_starts[-1] % 128
    if pad:
        gradients.append(jnp.zeros((dp, ring, rows, pad), bf16))
    grad_packed = jnp.concatenate(gradients, axis=3)
    dense_sum = dp_scatter([dp_block(grad_packed, k, dp, 0) for k in range(dp)], dp)[0]
    owned = lax.all_to_all(dense_sum.astype(bf16), "expert", 0, 0, tiled=True).astype(f32)

    def owned_field(number):
        return owned[..., grad_starts[number] : grad_starts[number + 1]]

    def heads_of(field):
        shared_field = field.reshape((head_groups, sharers) + field.shape[1:])
        return jnp.transpose(jnp.sum(shared_field, axis=1), (1, 0, 2))

    out_query = heads_of(owned_field(0)).reshape(rows, heads * QDIM)
    out_out = heads_of(owned_field(1)).reshape(rows, heads * VDIM).T
    out_up = heads_of(
        owned_field(2).reshape(ring, lat_rows, own_heads * KVDIM)
    ).reshape(lat_rows, heads * KVDIM)
    out_down = jnp.sum(owned_field(3), axis=0)
    out_router = jnp.sum(owned_field(4), axis=0)
    out_attn = jnp.sum(owned_field(5), axis=0).reshape(rows)
    out_moe = jnp.sum(owned_field(6), axis=0).reshape(rows)
    out_latent = jnp.sum(owned_field(7), axis=0)[:lat_rows].reshape(lat_rows)
    return (
        block_out,
        grad_tokens,
        out_attn,
        out_query,
        out_down,
        out_latent,
        out_up,
        out_out,
        out_moe,
        out_router,
        grad_shared_in_w[:, :shared_own],
        grad_shared_in_w[:, shared_own:],
        grad_shared_down,
        grad_expert_gate,
        grad_expert_up,
        grad_expert_down,
    )


def solution(mesh):
    both = ("dp", "expert")
    rows_first = P(both, None)
    vector = P(both)
    sequence = P(None, both, None)
    return jax.shard_map(
        per_device,
        mesh=mesh,
        in_specs=(
            sequence,
            sequence,
            P(),
            sequence,
            vector,
            rows_first,
            rows_first,
            vector,
            rows_first,
            P(None, both),
            vector,
            rows_first,
            P("dp", "expert"),
            P("dp", "expert"),
            P("expert", "dp"),
            P("expert", "dp", None),
            P("expert", "dp", None),
            P("expert", None, "dp"),
        ),
        out_specs=(
            sequence,
            sequence,
            vector,
            rows_first,
            rows_first,
            vector,
            rows_first,
            P(None, both),
            vector,
            rows_first,
            P("dp", "expert"),
            P("dp", "expert"),
            P("expert", "dp"),
            P("expert", "dp", None),
            P("expert", "dp", None),
            P("expert", None, "dp"),
        ),
        check_vma=False,
    )
```
